32 devices in a mesh: row: 4 (over y, core), col: 8 (over z, x).
Axes of the slice: x: 2, y: 2, z: 4, core: 2. Of those that a mesh axis runs over, the one named last changes fastest.
Arguments:
- probes: float32 [32768, 256], P(('row', 'col')), may hold values from -6 to 6
- near_blocks: bfloat16 [32, 8, 1024, 1024], P(('row', 'col')), may hold values from -0.09375 to 0.09375
- near_leaves: int32 [32, 8], P(('row', 'col')), may hold values from 0 to 7, as said below
- near_count: int32 [32], P(('row', 'col')), may hold values from 1 to 8, as said below
- leaf_rank: int32 [32], P(('row', 'col')), may hold values from 128 to 256
- leaf_basis: float32 [32768, 256], P(('row', 'col')), may hold values from -0.1875 to 0.1875
- leaf_transfer: float32 [32, 256, 512], P(('row', 'col')), may hold values from -0.125 to 0.125
- leaf_links: int32 [32, 4], P(('row', 'col')), may hold values from 0 to 7, as said below
- leaf_link_blocks: float32 [32, 4, 256, 256], P(('row', 'col')), may hold values from -0.1875 to 0.1875
- parent_links: int32 [4, 2], P('row'), may hold values from 0 to 3, as said below
- parent_link_blocks: float32 [4, 2, 512, 512], P('row'), may hold values from -0.1875 to 0.1875
Outputs:
- term_one: float32 [32768, 256], P(('row', 'col'))
- term_two: float32 [32768, 256], P(('row', 'col'))
The draws below stay inside these ranges and needn't reach their ends.
Inputs may be any that keep to these rules, and one draw needn't show every extreme that they name: `near_leaves`: slot 0 of every leaf is the leaf's own position; slots 1 to near_count - 1 are distinct other positions of the same group; later slots repeat the leaf's own position. `near_count`: some leaf has 8 live slots in every draw. `leaf_links`: each leaf's 4 coupled positions are distinct and differ from its own. `parent_links`: each parent's 2 coupled parents are distinct and differ from itself.
All inputs are finite; a program needn't handle non-finite values.
Results may differ from the reference program's by a relative error of at most 0.0034.
Values may be sent and summed in bfloat16 or wider, within the bound.
No kernel may reach another device: no remote copies, remote signals or barrier semaphores. Data moves between devices by JAX's collectives and lax.ppermute only.
A program may use at most 128 MiB of HBM per device.

```python
import jax
import jax.numpy as jnp
from jax import lax

LEAF = 1024
RANK_LEAF = 256
RANK_PARENT = 512
PROBES = 256
NEAR_MAX = 8
LC_MAX = 4
PC_MAX = 2
GROUPS = 4
GROUP_LEAVES = 8
LEAVES = 32
ORDER = 32768


def near_tables(key):
    base = jax.random.fold_in(key, 11)
    key_order = jax.random.fold_in(base, 1)
    key_count = jax.random.fold_in(base, 2)
    leaves = jnp.arange(LEAVES, dtype=jnp.int32)
    column = leaves % GROUP_LEAVES
    steps_away = jnp.arange(1, GROUP_LEAVES, dtype=jnp.int32)
    candidate = (column[:, None] + steps_away[None, :]) % GROUP_LEAVES
    scores = jax.random.randint(key_order, (LEAVES, GROUP_LEAVES - 1), 0, 1 << 20) * GROUP_LEAVES + steps_away[None, :]
    halfway = (steps_away == GROUP_LEAVES // 2)[None, :] & (leaves == 4)[:, None]
    scores = jnp.where(halfway, jnp.int32(-1), scores)
    ranking = jnp.argsort(scores, axis=1)
    picked = jnp.take_along_axis(candidate, ranking, axis=1)[:, :NEAR_MAX - 1]
    counts = jax.random.randint(key_count, (LEAVES,), 1, NEAR_MAX + 1)
    counts = counts.at[4].set(NEAR_MAX)
    listing = jnp.concatenate([column[:, None], picked], axis=1)
    slot_ids = jnp.arange(NEAR_MAX, dtype=jnp.int32)
    listing = jnp.where(slot_ids[None, :] < counts[:, None], listing, column[:, None])
    return (listing.astype(jnp.int32), counts.astype(jnp.int32))


def draw_near_leaves(key, part):
    return near_tables(key)[0]


def draw_near_count(key, part):
    return near_tables(key)[1]


def distinct_others(key, total, width, salt):
    base = jax.random.fold_in(key, salt)
    leaf_keys = jax.random.split(base, total)
    steps_away = jax.vmap(lambda leaf_key: jax.random.permutation(leaf_key, width - 1))(leaf_keys)
    return steps_away + 1


def draw_leaf_links(key, part):
    steps_away = distinct_others(key, LEAVES, GROUP_LEAVES, 23)[:, :LC_MAX]
    column = jnp.arange(LEAVES, dtype=jnp.int32) % GROUP_LEAVES
    return ((column[:, None] + steps_away) % GROUP_LEAVES).astype(jnp.int32)


def draw_parent_links(key, part):
    steps_away = distinct_others(key, GROUPS, GROUPS, 37)[:, :PC_MAX]
    owners = jnp.arange(GROUPS, dtype=jnp.int32)
    return ((owners[:, None] + steps_away) % GROUPS).astype(jnp.int32)


def with_ends(values, rng, smallest, largest):
    longest = values.shape.index(max(values.shape))
    spots = []
    for shift in (0, 1):
        where = [jax.random.randint(jax.random.fold_in(rng, axis), (), 0, length) for axis, length in enumerate(values.shape)]
        where[longest] = (where[longest] + shift) % values.shape[longest]
        spots.append(tuple(where))
    return values.at[spots[0]].set(smallest).at[spots[1]].set(largest)


def block_scale(rng, extent, shards, least, high):
    def one(position, blocks):
        heights = jax.random.uniform(jax.random.fold_in(jax.random.fold_in(rng, 6), position), (blocks,), jnp.float32, least / len(shards), high / len(shards))
        return jnp.repeat(jnp.exp(heights), extent[position] // blocks).reshape((-1,) + (1,) * (len(extent) - position - 1))

    factor_of = one(*shards[0])
    for cut in shards[1:]:
        factor_of = factor_of * one(*cut)
    return factor_of


def scatter_about(rng, extent, scale, limit, cuts=(), kind=jnp.bfloat16):
    array = scale * jax.random.normal(rng, extent, jnp.float32)
    if cuts:
        array = array * block_scale(rng, extent, cuts, -0.22, 0.18)
    return jnp.clip(array, -limit, limit).astype(kind)


def setup_inputs(seed: int = 0) -> dict:
    key_list = jax.random.split(jax.random.key(seed), 12)
    return {
        "probes": scatter_about(key_list[0], (ORDER, PROBES), 1.0, 6.0, ((0, 32),), jnp.float32),
        "near_blocks": scatter_about(key_list[1], (LEAVES, NEAR_MAX, LEAF, LEAF), (4 * LEAF) ** -0.5, 0.09375, ((0, 32),)),
        "near_leaves": draw_near_leaves(jax.random.fold_in(key_list[11], 71), 0),
        "near_count": draw_near_count(jax.random.fold_in(key_list[11], 71), 0),
        "leaf_rank": with_ends(jax.random.randint(key_list[4], (LEAVES,), RANK_LEAF // 2, RANK_LEAF + 1), jax.random.fold_in(key_list[4], 1), RANK_LEAF // 2, RANK_LEAF).astype(jnp.int32),
        "leaf_basis": scatter_about(key_list[5], (ORDER, RANK_LEAF), LEAF ** -0.5, 0.1875, ((0, 32),), jnp.float32),
        "leaf_transfer": scatter_about(key_list[6], (LEAVES, RANK_LEAF, RANK_PARENT), (RANK_LEAF * GROUP_LEAVES) ** -0.5, 0.125, ((0, 32),), jnp.float32),
        "leaf_links": draw_leaf_links(jax.random.fold_in(key_list[11], 71), 0),
        "leaf_link_blocks": scatter_about(key_list[8], (LEAVES, LC_MAX, RANK_LEAF, RANK_LEAF), (RANK_LEAF * LC_MAX) ** -0.5, 0.1875, ((0, 32),), jnp.float32),
        "parent_links": draw_parent_links(jax.random.fold_in(key_list[11], 71), 0),
        "parent_link_blocks": scatter_about(key_list[10], (GROUPS, PC_MAX, RANK_PARENT, RANK_PARENT), (RANK_PARENT * PC_MAX) ** -0.5, 0.1875, ((0, 4),), jnp.float32),
    }


def kernel_product(vector, near_blocks, near_leaves, near_count, leaf_rank, leaf_basis, leaf_transfer, leaf_links, leaf_link_blocks, parent_links, parent_link_blocks):
    highest = lax.Precision.HIGHEST
    owners = jnp.arange(LEAVES, dtype=jnp.int32) // GROUP_LEAVES
    packed = vector.astype(jnp.bfloat16).reshape(LEAVES, LEAF, PROBES)
    blocks_in = vector.reshape(LEAVES, LEAF, PROBES)
    basis = leaf_basis.reshape(LEAVES, LEAF, RANK_LEAF)
    rank_mask = (jnp.arange(RANK_LEAF, dtype=jnp.int32)[None, :] < leaf_rank[:, None]).astype(jnp.float32)[:, :, None]

    def near_leaf(leaf):
        sources = (owners[leaf] * GROUP_LEAVES + near_leaves[leaf]).astype(jnp.int32)

        def add_slot(slot, total):
            near_block = near_blocks[leaf, slot].astype(jnp.float32)
            source = packed[sources[slot]].astype(jnp.float32)
            return total + jnp.dot(near_block, source, precision=highest)

        return lax.fori_loop(0, near_count[leaf], add_slot, jnp.zeros((LEAF, PROBES), jnp.float32))

    near_sum = lax.map(near_leaf, jnp.arange(LEAVES, dtype=jnp.int32))
    skeleton = jnp.einsum('lir,lip->lrp', basis, blocks_in, precision=highest) * rank_mask
    linked = skeleton[(owners[:, None] * GROUP_LEAVES + leaf_links).astype(jnp.int32)]
    coupled = jnp.einsum('lkab,lkbp->lap', leaf_link_blocks, linked, precision=highest)
    upward = jnp.einsum('lrq,lrp->lqp', leaf_transfer, skeleton, precision=highest)
    parents = upward.reshape(GROUPS, GROUP_LEAVES, RANK_PARENT, PROBES).sum(axis=1)
    far_parent = jnp.einsum('gkab,gkbp->gap', parent_link_blocks, parents[parent_links], precision=highest)
    downward = jnp.einsum('lrq,lqp->lrp', leaf_transfer, far_parent[owners], precision=highest)
    combined = (coupled + downward) * rank_mask
    result = jnp.einsum('lir,lrp->lip', basis, combined, precision=highest) + near_sum
    return result.reshape(LEAVES * LEAF, PROBES)


def reference(probes, near_blocks, near_leaves, near_count, leaf_rank, leaf_basis, leaf_transfer, leaf_links, leaf_link_blocks, parent_links, parent_link_blocks):
    tables = (near_blocks, near_leaves, near_count, leaf_rank, leaf_basis, leaf_transfer, leaf_links, leaf_link_blocks, parent_links, parent_link_blocks)
    term_one = kernel_product(probes, *tables)
    term_two = 2.0 * kernel_product(term_one, *tables) - probes
    return term_one, term_two
```

```python
import functools

import jax
import jax.numpy as jnp
import numpy as np
from jax import lax
from jax.experimental import pallas as pl
from jax.experimental.pallas import tpu as pltpu
from jax.sharding import PartitionSpec as P


F32 = jnp.float32
BF16 = jnp.bfloat16
VMEM = pl.BlockSpec(memory_space=pltpu.VMEM)
SMEM = pl.BlockSpec(memory_space=pltpu.SMEM)


def ring_order(n):
    return list(range(0, n, 2)) + list(range(n - 1, 0, -2))


def halves(x):
    high = x.astype(BF16)
    low = (x - high.astype(F32)).astype(BF16)
    return high, low


def contract(a, b, dims):
    return lax.dot_general(a, b, (dims, ((), ())), preferred_element_type=F32)


def contract3(a, b, dims):
    a_high, a_low = halves(a)
    b_high, b_low = halves(b)
    small = contract(a_low, b_high, dims) + contract(a_high, b_low, dims)
    return small + contract(a_high, b_high, dims)


def contract2(a, b, dims):
    a_high, a_low = halves(a)
    return contract(a_low, b, dims) + contract(a_high, b, dims)


NN = ((1,), (0,))
NT = ((1,), (1,))
TN = ((0,), (0,))


def cost(flops, moved):
    return pl.CostEstimate(flops=int(flops), bytes_accessed=int(moved), transcendentals=0)


def front_body(rank_ref, v_ref, basis_ref, transfer_ref, message_ref, upward_ref):
    leaf_rows = v_ref.shape[0]
    rank_cols = basis_ref.shape[1]
    v = v_ref[...]
    skeleton = contract3(basis_ref[...], v, TN)
    row = lax.broadcasted_iota(jnp.int32, skeleton.shape, 0)
    skeleton = jnp.where(row < rank_ref[0], skeleton, 0.0)
    message_ref[:leaf_rows, :] = v.astype(BF16)
    message_ref[leaf_rows : leaf_rows + rank_cols, :] = skeleton.astype(BF16)
    upward_ref[...] = contract3(skeleton, transfer_ref[...], TN)


def front(v, basis, transfer, rank):
    leaf_rows, probe_cols = v.shape
    rank_cols, parent_cols = transfer.shape
    return pl.pallas_call(
        front_body,
        out_shape=(
            jax.ShapeDtypeStruct((leaf_rows + rank_cols, probe_cols), BF16),
            jax.ShapeDtypeStruct((probe_cols, parent_cols), F32),
        ),
        in_specs=[SMEM, VMEM, VMEM, VMEM],
        out_specs=(VMEM, VMEM),
        cost_estimate=cost(6 * leaf_rows * rank_cols * probe_cols, 8 * leaf_rows * probe_cols),
        name="front",
    )(rank, v, basis, transfer)


def own_body(block_ref, message_ref, out_ref):
    leaf_rows = block_ref.shape[2]
    out_ref[...] = contract(block_ref[0], message_ref[:leaf_rows, :], NN)


def own(blocks, message, tile):
    slots, leaf_rows, _ = blocks.shape
    probe_cols = message.shape[1]
    return pl.pallas_call(
        own_body,
        out_shape=jax.ShapeDtypeStruct((leaf_rows, probe_cols), F32),
        grid=(leaf_rows // tile,),
        in_specs=[
            pl.BlockSpec((1, tile, leaf_rows), lambda i: (0, i, 0)),
            pl.BlockSpec(message.shape, lambda i: (0, 0)),
        ],
        out_specs=pl.BlockSpec((tile, probe_cols), lambda i: (i, 0)),
        cost_estimate=cost(2 * leaf_rows * leaf_rows * probe_cols, 2 * leaf_rows * leaf_rows),
        name="own",
    )(blocks, message)


def absorb_body(first, tile, table_ref, near_ref, right_ref, left_ref, link_ref, near_in, coupled_in, near_out, coupled_out):
    side = pl.program_id(0)
    step = pl.program_id(1)
    leaf_rows = near_ref.shape[2]
    rows = pl.ds(pl.multiple_of(step * tile, tile), tile)

    def take(which, message_ref):
        slot = table_ref[0, first + which]
        link = table_ref[1, first + which]
        base = near_in if which == 0 else near_out

        @pl.when(slot >= 0)
        def _():
            near_out[rows, :] = base[rows, :] + contract(near_ref[0], message_ref[:leaf_rows, :], NN)

        if which == 0:

            @pl.when(slot < 0)
            def _():
                near_out[rows, :] = near_in[rows, :]

        @pl.when(step == 0)
        def _():
            if which == 0:
                coupled_out[...] = coupled_in[...]

            @pl.when(link >= 0)
            def _():
                coupled_out[...] += contract2(link_ref[jnp.maximum(link, 0)], message_ref[leaf_rows:, :], NN)

    @pl.when(side == 0)
    def _():
        take(0, right_ref)

    @pl.when(side == 1)
    def _():
        take(1, left_ref)


def absorb(table, first, blocks, right, left, links, near, coupled, tile):
    slots, leaf_rows, _ = blocks.shape
    probe_cols = right.shape[1]
    whole = lambda a: pl.BlockSpec(a.shape, lambda w, i, t: (0,) * a.ndim)
    return pl.pallas_call(
        functools.partial(absorb_body, first, tile),
        out_shape=(
            jax.ShapeDtypeStruct(near.shape, F32),
            jax.ShapeDtypeStruct(coupled.shape, F32),
        ),
        grid_spec=pltpu.PrefetchScalarGridSpec(
            num_scalar_prefetch=1,
            grid=(2, leaf_rows // tile),
            in_specs=[
                pl.BlockSpec(
                    (1, tile, leaf_rows), lambda w, i, t: (jnp.maximum(t[0, first + w], 0), i, 0)
                ),
                whole(right),
                whole(left),
                whole(links),
                whole(near),
                whole(coupled),
            ],
            out_specs=(whole(near), whole(coupled)),
        ),
        cost_estimate=cost(4 * leaf_rows * leaf_rows * probe_cols, 4 * leaf_rows * leaf_rows),
        name="absorb",
    )(table, blocks, right, left, links, near, coupled)


def far_body(count, links_ref, *refs):
    parents, blocks_ref, out_ref = refs[:count], refs[count], refs[count + 1]
    total = jnp.zeros(out_ref.shape, F32)
    for k in range(blocks_ref.shape[0]):
        chosen = parents[0][...]
        for e in range(1, count):
            chosen = jnp.where(links_ref[k] == e, parents[e][...], chosen)
        high, low = halves(blocks_ref[k])
        total += contract(chosen, low, NT) + contract(chosen, high, NT)
    out_ref[...] = total.astype(BF16)


def far_share(links, parents, blocks):
    return pl.pallas_call(
        functools.partial(far_body, len(parents)),
        out_shape=jax.ShapeDtypeStruct(parents[0].shape, BF16),
        in_specs=[SMEM] + [VMEM] * (len(parents) + 1),
        out_specs=VMEM,
        cost_estimate=cost(2**24, blocks.size * 4),
        name="far",
    )(links, *parents, blocks)


def back_body(final, first, tile, table_ref, rank_ref, near_ref, top_ref, bottom_ref, link_ref, acc_ref, coupled_ref, far_ref, transfer_ref, basis_ref, *rest):
    if final:
        start_ref, out_ref, combined_ref = rest
    else:
        out_ref, combined_ref = rest
    step = pl.program_id(0)
    leaf_rows = near_ref.shape[2]
    half = top_ref.shape[0]
    tail = leaf_rows - half
    slot = table_ref[0, first]
    link = table_ref[1, first]
    rows = pl.ds(pl.multiple_of(step * tile, tile), tile)

    @pl.when(step == 0)
    def _():
        combined_ref[...] = coupled_ref[...] + contract2(transfer_ref[...], far_ref[...], NT)

        @pl.when(link >= 0)
        def _():
            combined_ref[...] += contract2(link_ref[jnp.maximum(link, 0)], bottom_ref[tail:, :], NN)

        row = lax.broadcasted_iota(jnp.int32, combined_ref.shape, 0)
        combined_ref[...] = jnp.where(row < rank_ref[0], combined_ref[...], 0.0)

    value = acc_ref[rows, :] + contract3(basis_ref[rows, :], combined_ref[...], NN)
    if final:
        out_ref[...] = 2.0 * value - start_ref[rows, :]
    else:
        out_ref[...] = value

    @pl.when(slot >= 0)
    def _():
        more = contract(near_ref[0, :, :half], top_ref[...], NN)
        more += contract(near_ref[0, :, half:], bottom_ref[:tail, :], NN)
        if final:
            more = 2.0 * more
        out_ref[...] += more


def back(table, first, rank, blocks, top, bottom, links, near, coupled, far, transfer, basis, start, tile):
    slots, leaf_rows, _ = blocks.shape
    probe_cols = top.shape[1]
    final = start is not None
    whole = lambda a: pl.BlockSpec(a.shape, lambda i, *t: (0,) * a.ndim)
    operands = [blocks, top, bottom, links, near, coupled, far, transfer, basis] + ([start] if final else [])
    return pl.pallas_call(
        functools.partial(back_body, final, first, tile),
        out_shape=jax.ShapeDtypeStruct(near.shape, F32),
        grid_spec=pltpu.PrefetchScalarGridSpec(
            num_scalar_prefetch=2,
            grid=(leaf_rows // tile,),
            in_specs=[
                pl.BlockSpec(
                    (1, tile, leaf_rows), lambda i, t, r: (jnp.maximum(t[0, first], 0), i, 0)
                )
            ]
            + [whole(a) for a in operands[1:]],
            out_specs=pl.BlockSpec((tile, probe_cols), lambda i, *t: (i, 0)),
            scratch_shapes=[pltpu.VMEM(coupled.shape, F32)],
        ),
        cost_estimate=cost(4 * leaf_rows * leaf_rows * probe_cols, 4 * leaf_rows * leaf_rows),
        name="back",
    )(table, rank, *operands)


def local(
    probes,
    near_blocks,
    near_leaves,
    near_count,
    leaf_rank,
    leaf_basis,
    leaf_transfer,
    leaf_links,
    leaf_link_blocks,
    parent_links,
    parent_link_blocks,
):
    n = lax.axis_size("col")
    span_row = lax.axis_size("row")
    me = lax.axis_index("col")
    my_row = lax.axis_index("row")
    leaf_rows, probe_cols = probes.shape
    tile = leaf_rows // 2
    transfer = leaf_transfer[0]
    blocks = near_blocks[0]
    link_blocks = leaf_link_blocks[0]
    bits = n.bit_length() - 1
    assert 1 << bits == n

    order = ring_order(n)
    place = {leaf: at for at, leaf in enumerate(order)}
    to_right = [(order[i], order[(i + 1) % n]) for i in range(n)]
    to_left = [(b, a) for a, b in to_right]
    steps = n // 2 - 1

    arrivals = np.zeros((n, n - 1), np.int32)
    for c in range(n):
        for s in range(steps):
            arrivals[c, 2 * s] = order[(place[c] - s - 1) % n]
            arrivals[c, 2 * s + 1] = order[(place[c] + s + 1) % n]
        arrivals[c, n - 2] = order[(place[c] + n // 2) % n]
    source = lax.dynamic_index_in_dim(jnp.asarray(arrivals), me, 0, False)
    slot_ids = jnp.arange(near_leaves.shape[1], dtype=jnp.int32)[:, None]
    live = (near_leaves[0][:, None] == source[None, :]) & (slot_ids < near_count[0])
    link_ids = jnp.arange(leaf_links.shape[1], dtype=jnp.int32)[:, None]
    linked = leaf_links[0][:, None] == source[None, :]
    table = jnp.stack(
        [
            jnp.max(jnp.where(live, slot_ids, -1), axis=0),
            jnp.max(jnp.where(linked, link_ids, -1), axis=0),
        ]
    )
    far_links = jnp.bitwise_xor(parent_links[0], my_row)

    def swap(value, axis, size, distance):
        return lax.ppermute(value, axis, [(i, i ^ distance) for i in range(size)])

    def multiply(vector, start):
        message, upward = front(vector, leaf_basis, transfer, leaf_rank)
        right = lax.ppermute(message, "col", to_right)
        left = lax.ppermute(message, "col", to_left)

        total = upward
        for b in range(bits):
            pair = total.reshape(2, total.shape[0] // 2, total.shape[1])
            bit = (me >> b) & 1
            away = lax.dynamic_index_in_dim(pair, 1 - bit, 0, False).astype(BF16)
            kept = lax.dynamic_index_in_dim(pair, bit, 0, False)
            total = kept + swap(away, "col", n, 1 << b).astype(F32)
        share = total.astype(BF16)
        parents = [share] + [swap(share, "row", span_row, e) for e in range(1, span_row)]
        far = far_share(far_links, parents, parent_link_blocks[0])
        for b in reversed(range(bits)):
            bit = (me >> b) & 1
            other = swap(far, "col", n, 1 << b)
            far = jnp.where(bit == 0, jnp.concatenate([far, other]), jnp.concatenate([other, far]))

        near = own(blocks, message, tile)
        coupled = jnp.zeros((leaf_basis.shape[1], probe_cols), F32)
        for s in range(steps):
            if s + 1 < steps:
                next_right = lax.ppermute(right, "col", to_right)
                next_left = lax.ppermute(left, "col", to_left)
            else:
                half = right.shape[0] // 2
                next_right = lax.ppermute(right[:half], "col", to_right)
                next_left = lax.ppermute(left[half:], "col", to_left)
            near, coupled = absorb(
                table, 2 * s, blocks, right, left, link_blocks, near, coupled, tile
            )
            right, left = next_right, next_left
        return back(
            table, n - 2, leaf_rank, blocks, right, left, link_blocks, near, coupled, far,
            transfer, leaf_basis, start, tile,
        )

    term_one = multiply(probes, None)
    term_two = multiply(term_one, probes)
    return (term_one, term_two)


def solution(mesh):
    in_specs = (
        P(("row", "col"), None),
        P(("row", "col"), None, None, None),
        P(("row", "col"), None),
        P(("row", "col")),
        P(("row", "col")),
        P(("row", "col"), None),
        P(("row", "col"), None, None),
        P(("row", "col"), None),
        P(("row", "col"), None, None, None),
        P("row", None),
        P("row", None, None, None),
    )
    out_specs = (P(("row", "col"), None), P(("row", "col"), None))
    return jax.shard_map(local, mesh=mesh, in_specs=in_specs, out_specs=out_specs, check_vma=False)
```

```python
import functools

import jax
import jax.numpy as jnp
from jax import lax
from jax.experimental import pallas as pl
from jax.experimental.pallas import tpu as pltpu
from jax.sharding import PartitionSpec as P


F32 = jnp.float32
BF16 = jnp.bfloat16
VMEM = pl.BlockSpec(memory_space=pltpu.VMEM)
SMEM = pl.BlockSpec(memory_space=pltpu.SMEM)


def ring_order(n):
    return list(range(0, n, 2)) + list(range(n - 1, 0, -2))


def halves(x):
    high = x.astype(BF16)
    low = (x - high.astype(F32)).astype(BF16)
    return high, low


def contract(a, b, dims):
    return lax.dot_general(a, b, (dims, ((), ())), preferred_element_type=F32)


def contract3(a, b, dims):
    a_high, a_low = halves(a)
    b_high, b_low = halves(b)
    small = contract(a_low, b_high, dims) + contract(a_high, b_low, dims)
    return small + contract(a_high, b_high, dims)


def contract2(a, b, dims):
    a_high, a_low = halves(a)
    return contract(a_low, b, dims) + contract(a_high, b, dims)


NN = ((1,), (0,))
NT = ((1,), (1,))
TN = ((0,), (0,))


def cost(flops, moved):
    return pl.CostEstimate(flops=int(flops), bytes_accessed=int(moved), transcendentals=0)


def share_of(me, bits):
    share = me & 1
    for b in range(1, bits):
        share = 2 * share + ((me >> b) & 1)
    return share


def front_body(me_ref, rank_ref, v_ref, basis_ref, transfer_ref, bottom_ref, away_ref, kept_ref, upward_ref):
    leaf_rows = v_ref.shape[0]
    part = bottom_ref.shape[0]
    v = v_ref[...]
    skeleton = contract3(basis_ref[...], v, TN)
    row = lax.broadcasted_iota(jnp.int32, skeleton.shape, 0)
    skeleton = jnp.where(row < rank_ref[0], skeleton, 0.0)
    bottom_ref[: leaf_rows - part, :] = v[part:, :].astype(BF16)
    bottom_ref[leaf_rows - part :, :] = skeleton.astype(BF16)
    upward_ref[...] = contract3(skeleton, transfer_ref[...], TN)
    half = kept_ref.shape[0]
    bit = me_ref[0] & 1
    away_ref[...] = upward_ref[pl.ds(pl.multiple_of((1 - bit) * half, half), half), :].astype(BF16)
    kept_ref[...] = upward_ref[pl.ds(pl.multiple_of(bit * half, half), half), :]


def front(me, v, basis, transfer, rank):
    leaf_rows, probe_cols = v.shape
    rank_cols, parent_cols = transfer.shape
    part = (leaf_rows + rank_cols) // 2
    return pl.pallas_call(
        front_body,
        out_shape=(
            jax.ShapeDtypeStruct((part, probe_cols), BF16),
            jax.ShapeDtypeStruct((probe_cols // 2, parent_cols), BF16),
            jax.ShapeDtypeStruct((probe_cols // 2, parent_cols), F32),
        ),
        in_specs=[SMEM, SMEM, VMEM, VMEM, VMEM],
        out_specs=(VMEM,) * 3,
        scratch_shapes=[pltpu.VMEM((probe_cols, parent_cols), F32)],
        cost_estimate=cost(6 * v.size * rank_cols, 8 * v.size),
        name="front",
    )(me, rank, v, basis, transfer)


ANY = pl.BlockSpec(memory_space=pl.ANY)


DEPTH = 3


class Copies:
    def __init__(self, sems):
        self.sems = sems
        self.made = []

    def start(self, source, target, when=None):
        copy = pltpu.make_async_copy(source, target, self.sems.at[len(self.made)])
        self.made.append(copy)
        if when is None:
            copy.start()
        else:
            pl.when(when)(copy.start)
        return copy


def origin(me, j, n):
    place = jnp.where(me & 1 == 1, n - ((me + 1) >> 1), me >> 1)
    step = (j + 1) // 2
    place = place - step if j % 2 else place + step
    place = jnp.where(place < 0, place + n, jnp.where(place >= n, place - n, place))
    return jnp.where(place < n // 2, 2 * place, 2 * (n - place) - 1)


def named(me_ref, near_ref, count_ref, links_ref, j, n):
    leaf = origin(me_ref[0], j, n)
    slot = jnp.int32(-1)
    for k in range(near_ref.shape[1]):
        slot = jnp.where((near_ref[0, k] == leaf) & (k < count_ref[0]), k, slot)
    link = jnp.int32(-1)
    for k in range(links_ref.shape[1]):
        link = jnp.where(links_ref[0, k] == leaf, k, link)
    return slot >= 0, jnp.maximum(slot, 0), link >= 0, jnp.maximum(link, 0)


def absorb(tables, n, first, blocks, links, messages, sums):
    leaf_rows = blocks.shape[1]
    rank_cols = links.shape[1]
    part, probe_cols = messages[0][0].shape
    count = len(messages)
    outs = (
        jax.ShapeDtypeStruct((leaf_rows, probe_cols), F32),
        jax.ShapeDtypeStruct((rank_cols, probe_cols), F32),
    )
    operands = [p for message in messages for p in message] + list(sums)

    def body(me_ref, nears_ref, count_ref, ties_ref, blocks_ref, links_ref, *refs):
        near_out, coupled_out, block_ref, link_ref, held_ref, sems = refs[len(operands) :]
        copies = Copies(sems)

        def fetch(j):
            at = j % DEPTH
            live, slot, linked, link = named(me_ref, nears_ref, count_ref, ties_ref, first + j, n)
            got = [copies.start(refs[2 * j + c], held_ref.at[at, pl.ds(c * part, part)]) for c in (0, 1)]
            block = copies.start(blocks_ref.at[slot], block_ref.at[at], live)
            tie = copies.start(links_ref.at[link], link_ref.at[at], linked)
            return live, linked, got, block, tie

        if sums:
            base = [copies.start(refs[2 * count], near_out), copies.start(refs[2 * count + 1], coupled_out)]
        fetched = [fetch(j) for j in range(min(count, DEPTH - 1))]
        if sums:
            for copy in base:
                copy.wait()
        else:
            near_out[...] = jnp.zeros_like(near_out)
            coupled_out[...] = jnp.zeros_like(coupled_out)
        for j in range(count):
            live, linked, got, block, tie = fetched[j]
            at = j % DEPTH
            for copy in got:
                copy.wait()
            pl.when(live)(block.wait)
            if j + DEPTH - 1 < count:
                fetched.append(fetch(j + DEPTH - 1))

            @pl.when(live)
            def _():
                near_out[...] += contract(block_ref[at], held_ref[at, :leaf_rows, :], NN)

            @pl.when(linked)
            def _():
                tie.wait()
                coupled_out[...] += contract2(link_ref[at], held_ref[at, leaf_rows:, :], NN)

    return pl.pallas_call(
        body,
        out_shape=outs,
        in_specs=[SMEM] * 4 + [ANY] * (2 + len(operands)),
        out_specs=(VMEM, VMEM),
        scratch_shapes=[
            pltpu.VMEM((DEPTH,) + blocks.shape[1:], BF16),
            pltpu.VMEM((DEPTH,) + links.shape[1:], F32),
            pltpu.VMEM((DEPTH, 2 * part, probe_cols), BF16),
            pltpu.SemaphoreType.DMA((4 * count + 2,)),
        ],
        cost_estimate=cost(2 * count * blocks[0].size * probe_cols, 4 * count * blocks[0].size),
        name="absorb",
    )(*tables, blocks, links, *operands)


def far_body(count, row_ref, links_ref, *refs):
    parents, blocks_ref, out_ref = refs[:count], refs[count], refs[count + 1]
    total = jnp.zeros(out_ref.shape, F32)
    for k in range(blocks_ref.shape[0]):
        chosen = parents[0][...]
        away = jnp.bitwise_xor(links_ref[0, k], row_ref[0])
        for e in range(1, count):
            chosen = jnp.where(away == e, parents[e][...], chosen)
        high, low = halves(blocks_ref[k])
        total += contract(chosen, low, NT) + contract(chosen, high, NT)
    out_ref[...] = total.astype(BF16)


def far_share(row, links, parents, blocks):
    return pl.pallas_call(
        functools.partial(far_body, len(parents)),
        out_shape=jax.ShapeDtypeStruct(parents[0].shape, BF16),
        in_specs=[SMEM, SMEM] + [VMEM] * (len(parents) + 1),
        out_specs=VMEM,
        cost_estimate=cost(2**24, blocks.size * 4),
        name="far",
    )(row, links, *parents, blocks)


def far_bits(far):
    total = sum(piece.shape[0] for piece in far) // far[0].shape[0]
    return total.bit_length() - 1


def reversed_bits(at, bits):
    return sum(((at >> b) & 1) << (bits - 1 - b) for b in range(bits))


def back(tables, n, rank, blocks, links, parts, near, coupled, far, transfer, basis, start):
    leaf_rows = blocks.shape[1]
    half = leaf_rows // 2
    final = start is not None
    part = parts[0].shape[0]
    count = len(far)
    bits = far_bits(far)
    operands = list(far) + [transfer, coupled, *parts, basis, near] + ([start] if final else [])

    def body(me_ref, nears_ref, count_ref, ties_ref, rank_ref, blocks_ref, links_ref, *refs):
        far_refs = refs[:count]
        transfer_in, coupled_in, top_ref, bottom_ref, basis_in, near_in = refs[count : count + 6]
        rest = refs[len(operands) :]
        out_ref, *sent_refs = rest[: 1 if final else 2]
        transfer_ref, basis_ref, block_ref, link_ref, held_ref, spread_ref, combined_ref = rest[
            len(sent_refs) + 1 : len(sent_refs) + 8
        ]
        sems = rest[-1]
        copies = Copies(sems)
        live, slot, linked, link = named(me_ref, nears_ref, count_ref, ties_ref, n - 1, n)
        rows = far_refs[0].shape[0]
        early = []
        at = 0
        for ref in far_refs:
            for piece in range(ref.shape[0] // rows):
                share = share_of(jnp.bitwise_xor(me_ref[0], reversed_bits(at, bits)), bits)
                early.append(
                    copies.start(
                        ref.at[pl.ds(piece * rows, rows)],
                        spread_ref.at[pl.ds(pl.multiple_of(share * rows, rows), rows)],
                    )
                )
                at += 1
        early.append(copies.start(transfer_in, transfer_ref))
        early.append(copies.start(coupled_in, combined_ref))
        bottom = copies.start(bottom_ref, held_ref.at[pl.ds(part, part)])
        tie = copies.start(links_ref.at[link], link_ref, linked)
        basis_copy = copies.start(basis_in, basis_ref)
        base = copies.start(near_in, out_ref)
        for copy in early:
            copy.wait()
        top = copies.start(top_ref, held_ref.at[pl.ds(0, part)])
        ready = [
            copies.start(
                blocks_ref.at[slot, pl.ds(c * half, half)], block_ref.at[pl.ds(c * half, half)], live
            )
            for c in (0, 1)
        ]
        if final:
            past = copies.start(refs[len(operands) - 1], rest[-2])

        combined_ref[...] += contract2(transfer_ref[...], spread_ref[...], NT)
        bottom.wait()

        @pl.when(linked)
        def _():
            tie.wait()
            combined_ref[...] += contract2(link_ref[...], held_ref[leaf_rows:, :], NN)

        row = lax.broadcasted_iota(jnp.int32, combined_ref.shape, 0)
        combined = jnp.where(row < rank_ref[0], combined_ref[...], 0.0)
        basis_copy.wait()
        base.wait()
        out_ref[...] += contract3(basis_ref[...], combined, NN)
        top.wait()

        @pl.when(live)
        def _():
            for c in (0, 1):
                ready[c].wait()
                at = pl.ds(c * half, half)
                out_ref[at, :] += contract(block_ref[at, :], held_ref[:leaf_rows, :], NN)

        if final:
            past.wait()
            out_ref[...] = 2.0 * out_ref[...] - rest[-2][...]
        else:
            sent_refs[0][...] = out_ref[:part, :].astype(BF16)

    out = jax.ShapeDtypeStruct(near.shape, F32)
    outs = (out,) if final else (out, jax.ShapeDtypeStruct(parts[0].shape, BF16))
    return pl.pallas_call(
        body,
        out_shape=outs,
        in_specs=[SMEM] * 5 + [ANY] * (2 + len(operands)),
        out_specs=(VMEM,) * len(outs),
        scratch_shapes=[
            pltpu.VMEM(transfer.shape, F32),
            pltpu.VMEM(basis.shape, F32),
            pltpu.VMEM(blocks.shape[1:], BF16),
            pltpu.VMEM(links.shape[1:], F32),
            pltpu.VMEM((2 * part, near.shape[1]), BF16),
            pltpu.VMEM((near.shape[1], transfer.shape[1]), BF16),
            pltpu.VMEM(coupled.shape, F32),
        ]
        + ([pltpu.VMEM(near.shape, F32)] if final else [])
        + [pltpu.SemaphoreType.DMA((12 + (1 << bits),))],
        cost_estimate=cost(6 * blocks[0].size * near.shape[1], 6 * blocks[0].size),
        name="back",
    )(*tables, rank, blocks, links, *operands)


def local(
    probes,
    near_blocks,
    near_leaves,
    near_count,
    leaf_rank,
    leaf_basis,
    leaf_transfer,
    leaf_links,
    leaf_link_blocks,
    parent_links,
    parent_link_blocks,
):
    n = lax.axis_size("col")
    span_row = lax.axis_size("row")
    me = lax.axis_index("col")
    my_row = lax.axis_index("row")
    leaf_rows, _ = probes.shape
    transfer = leaf_transfer[0]
    blocks = near_blocks[0]
    link_blocks = leaf_link_blocks[0]
    bits = n.bit_length() - 1
    assert 1 << bits == n

    order = ring_order(n)
    to_right = [(order[i], order[(i + 1) % n]) for i in range(n)]
    to_left = [(b, a) for a, b in to_right]
    steps = n // 2 - 1

    mine = jnp.reshape(me, (1,))
    tables = (mine, near_leaves, near_count, leaf_links)

    def swap(value, axis, size, distance):
        return lax.ppermute(value, axis, [(i, i ^ distance) for i in range(size)])

    def pass_on(value, perm):
        return lax.ppermute(value, "col", perm)

    def multiply(vector, top, start):
        bottom, away, kept = front(mine, vector, leaf_basis, transfer, leaf_rank)

        for b in range(bits):
            if b:
                pair = total.reshape(2, total.shape[0] // 2, total.shape[1])
                bit = (me >> b) & 1
                away = lax.dynamic_index_in_dim(pair, 1 - bit, 0, False).astype(BF16)
                kept = lax.dynamic_index_in_dim(pair, bit, 0, False)
            total = kept + swap(away, "col", n, 1 << b).astype(F32)
        share = total.astype(BF16)
        parents = [share] + [swap(share, "row", span_row, e) for e in range(1, span_row)]
        far = [far_share(jnp.reshape(my_row, (1,)), parent_links, parents, parent_link_blocks[0])]
        for b in reversed(range(bits)):
            held = far[0] if len(far) == 1 else jnp.concatenate(far)
            far.append(swap(held, "col", n, 1 << b))

        messages = [(top, bottom)]
        right = left = (top, bottom)
        for _ in range(1, steps + 1):
            right = tuple(pass_on(right[c], to_right) for c in (0, 1))
            left = tuple(pass_on(left[c], to_left) for c in (0, 1))
            messages += [right, left]
        opposite = (pass_on(right[0], to_right), pass_on(left[1], to_left))
        sums = ()
        first = 0
        for s in range(1, steps + 1):
            taken = messages[first : 2 * s + 1]
            sums = absorb(tables, n, first, blocks, link_blocks, taken, sums)
            first = 2 * s + 1
        return back(
            tables, n, leaf_rank, blocks, link_blocks, opposite, *sums, far,
            transfer, leaf_basis, start,
        )

    part = (leaf_rows + leaf_basis.shape[1]) // 2
    term_one, top = multiply(probes, probes[:part].astype(BF16), None)
    (term_two,) = multiply(term_one, top, probes)
    return (term_one, term_two)


def solution(mesh):
    in_specs = (
        P(("row", "col"), None),
        P(("row", "col"), None, None, None),
        P(("row", "col"), None),
        P(("row", "col")),
        P(("row", "col")),
        P(("row", "col"), None),
        P(("row", "col"), None, None),
        P(("row", "col"), None),
        P(("row", "col"), None, None, None),
        P("row", None),
        P("row", None, None, None),
    )
    out_specs = (P(("row", "col"), None), P(("row", "col"), None))
    return jax.shard_map(local, mesh=mesh, in_specs=in_specs, out_specs=out_specs, check_vma=False)
```

```python
import jax
import jax.numpy as jnp
from jax import lax
from jax.experimental import pallas as pl
from jax.experimental.pallas import tpu as pltpu
from jax.sharding import PartitionSpec as P


F32 = jnp.float32
BF16 = jnp.bfloat16
VMEM = pl.BlockSpec(memory_space=pltpu.VMEM)
SMEM = pl.BlockSpec(memory_space=pltpu.SMEM)
HBM = pl.BlockSpec(memory_space=pltpu.HBM)
ANY = pl.BlockSpec(memory_space=pl.ANY)
ROOM = pltpu.CompilerParams(vmem_limit_bytes=24 * 2**20)


def ring_order(n):
    return list(range(0, n, 2)) + list(range(n - 1, 0, -2))


def halves(x):
    high = x.astype(BF16)
    low = (x - high.astype(F32)).astype(BF16)
    return high, low


def contract(a, b, dims):
    return lax.dot_general(a, b, (dims, ((), ())), preferred_element_type=F32)


def contract3(a, b, dims):
    a_high, a_low = halves(a)
    b_high, b_low = halves(b)
    small = contract(a_low, b_high, dims) + contract(a_high, b_low, dims)
    return small + contract(a_high, b_high, dims)


def contract2(a, b, dims):
    a_high, a_low = halves(a)
    return contract(a_low, b, dims) + contract(a_high, b, dims)


NN = ((1,), (0,))
NT = ((1,), (1,))
TN = ((0,), (0,))


def cost(flops, moved):
    return pl.CostEstimate(flops=int(flops), bytes_accessed=int(moved), transcendentals=0)


def share_of(me, bits):
    share = me & 1
    for b in range(1, bits):
        share = 2 * share + ((me >> b) & 1)
    return share


DEPTH = 3


class Copies:
    def __init__(self, sems):
        self.sems = sems
        self.made = []

    def start(self, source, target, when=None):
        copy = pltpu.make_async_copy(source, target, self.sems.at[len(self.made)])
        self.made.append(copy)
        if when is None:
            copy.start()
        else:
            pl.when(when)(copy.start)
        return copy


def front(me, v, basis, transfer, rank):
    leaf_rows, probe_cols = v.shape
    rank_cols, parent_cols = transfer.shape
    part = (leaf_rows + rank_cols) // 2
    half = probe_cols // 2

    def body(me_ref, rank_ref, v_in, basis_in, transfer_in, bottom_ref, away_ref, kept_ref, v_ref, basis_ref, transfer_ref, upward_ref, sems):
        copies = Copies(sems)
        first = [copies.start(v_in, v_ref), copies.start(basis_in, basis_ref)]
        last = copies.start(transfer_in, transfer_ref)
        for copy in first:
            copy.wait()
        v = v_ref[...]
        skeleton = contract3(basis_ref[...], v, TN)
        row = lax.broadcasted_iota(jnp.int32, skeleton.shape, 0)
        skeleton = jnp.where(row < rank_ref[0], skeleton, 0.0)
        bottom_ref[: leaf_rows - part, :] = v[part:, :].astype(BF16)
        bottom_ref[leaf_rows - part :, :] = skeleton.astype(BF16)
        last.wait()
        upward_ref[...] = contract3(skeleton, transfer_ref[...], TN)
        bit = me_ref[0] & 1
        away_ref[...] = upward_ref[pl.ds(pl.multiple_of((1 - bit) * half, half), half), :].astype(BF16)
        kept_ref[...] = upward_ref[pl.ds(pl.multiple_of(bit * half, half), half), :]

    return pl.pallas_call(
        body,
        out_shape=(
            jax.ShapeDtypeStruct((part, probe_cols), BF16),
            jax.ShapeDtypeStruct((half, parent_cols), BF16),
            jax.ShapeDtypeStruct((half, parent_cols), F32),
        ),
        in_specs=[SMEM, SMEM, HBM, HBM, HBM],
        out_specs=(VMEM,) * 3,
        scratch_shapes=[
            pltpu.VMEM(v.shape, F32),
            pltpu.VMEM(basis.shape, F32),
            pltpu.VMEM(transfer.shape, F32),
            pltpu.VMEM((probe_cols, parent_cols), F32),
            pltpu.SemaphoreType.DMA((3,)),
        ],
        cost_estimate=cost(6 * v.size * rank_cols, 8 * v.size),
        compiler_params=ROOM,
        name="front",
    )(me, rank, v, basis, transfer)


def origin(me, j, n):
    place = jnp.where(me & 1 == 1, n - ((me + 1) >> 1), me >> 1)
    step = (j + 1) // 2
    place = place - step if j % 2 else place + step
    place = jnp.where(place < 0, place + n, jnp.where(place >= n, place - n, place))
    return jnp.where(place < n // 2, 2 * place, 2 * (n - place) - 1)


def named(me_ref, near_ref, count_ref, links_ref, j, n):
    leaf = origin(me_ref[0], j, n)
    slot = jnp.int32(-1)
    for k in range(near_ref.shape[1]):
        slot = jnp.where((near_ref[0, k] == leaf) & (k < count_ref[0]), k, slot)
    link = jnp.int32(-1)
    for k in range(links_ref.shape[1]):
        link = jnp.where(links_ref[0, k] == leaf, k, link)
    return slot >= 0, jnp.maximum(slot, 0), link >= 0, jnp.maximum(link, 0)


def take_all(tables, n, first, count, copies, blocks_ref, links_ref, parts, held, near_ref, coupled_ref):
    block_ref, link_ref, held_ref = held
    part = parts[0].shape[0]
    leaf_rows = near_ref.shape[0]

    def fetch(j):
        at = j % DEPTH
        live, slot, linked, link = named(*tables, first + j, n)
        got = [copies.start(parts[2 * j + c], held_ref.at[at, pl.ds(c * part, part)]) for c in (0, 1)]
        block = copies.start(blocks_ref.at[slot], block_ref.at[at], live)
        tie = copies.start(links_ref.at[link], link_ref.at[at], linked)
        return live, linked, got, block, tie

    fetched = [fetch(j) for j in range(min(count, DEPTH - 1))]
    yield
    for j in range(count):
        live, linked, got, block, tie = fetched[j]
        at = j % DEPTH
        for copy in got:
            copy.wait()
        pl.when(live)(block.wait)
        if j + DEPTH - 1 < count:
            fetched.append(fetch(j + DEPTH - 1))
        yield

        @pl.when(live)
        def _():
            near_ref[...] += contract(block_ref[at], held_ref[at, :leaf_rows, :], NN)

        @pl.when(linked)
        def _():
            tie.wait()
            coupled_ref[...] += contract2(link_ref[at], held_ref[at, leaf_rows:, :], NN)


def held_scratch(blocks, links, part):
    return [
        pltpu.VMEM((DEPTH,) + blocks.shape[1:], BF16),
        pltpu.VMEM((DEPTH,) + links.shape[1:], F32),
        pltpu.VMEM((DEPTH, 2 * part.shape[0], part.shape[1]), BF16),
    ]


def absorb(tables, n, first, blocks, links, messages, sums):
    probe_cols = messages[0][0].shape[1]
    count = len(messages)
    outs = (
        jax.ShapeDtypeStruct((blocks.shape[1], probe_cols), F32),
        jax.ShapeDtypeStruct((links.shape[1], probe_cols), F32),
    )
    operands = [p for message in messages for p in message] + list(sums)

    def body(*refs):
        tables_in, blocks_ref, links_ref, refs = refs[:4], refs[4], refs[5], refs[6:]
        near_out, coupled_out, *held, sems = refs[len(operands) :]
        copies = Copies(sems)
        base = [
            copies.start(given, out)
            for given, out in zip(refs[2 * count : len(operands)], (near_out, coupled_out))
        ]
        work = take_all(
            tables_in, n, first, count, copies, blocks_ref, links_ref, refs[: 2 * count], held,
            near_out, coupled_out,
        )
        next(work)
        if sums:
            for copy in base:
                copy.wait()
        else:
            near_out[...] = jnp.zeros_like(near_out)
            coupled_out[...] = jnp.zeros_like(coupled_out)
        for _ in work:
            pass

    return pl.pallas_call(
        body,
        out_shape=outs,
        in_specs=[SMEM] * 4 + [HBM] * 2 + [ANY] * len(operands),
        out_specs=(VMEM, VMEM),
        scratch_shapes=held_scratch(blocks, links, messages[0][0])
        + [pltpu.SemaphoreType.DMA((4 * count + 2,))],
        cost_estimate=cost(2 * count * (blocks.shape[1] ** 2) * probe_cols, 4 * count * (blocks.shape[1] ** 2)),
        compiler_params=ROOM,
        name="absorb",
    )(*tables, blocks, links, *operands)


def far_share(row, links, parents, blocks):
    count = len(parents)
    slots = blocks.shape[0]

    def body(row_ref, links_ref, *refs):
        blocks_in, out_ref, blocks_ref, parents_ref, sems = refs[count:]
        copies = Copies(sems)
        brought = [copies.start(refs[e], parents_ref.at[e]) for e in range(count)]
        fetched = [copies.start(blocks_in.at[k], blocks_ref.at[k]) for k in range(slots)]
        for copy in brought:
            copy.wait()
        total = jnp.zeros(out_ref.shape, F32)
        for k in range(slots):
            away = jnp.bitwise_xor(links_ref[0, k], row_ref[0])
            chosen = parents_ref[away]
            fetched[k].wait()
            high, low = halves(blocks_ref[k])
            total += contract(chosen, low, NT) + contract(chosen, high, NT)
        out_ref[...] = total.astype(BF16)

    return pl.pallas_call(
        body,
        out_shape=jax.ShapeDtypeStruct(parents[0].shape, BF16),
        in_specs=[SMEM, SMEM] + [ANY] * count + [HBM],
        out_specs=VMEM,
        scratch_shapes=[
            pltpu.VMEM(blocks.shape, F32),
            pltpu.VMEM((count,) + parents[0].shape, BF16),
            pltpu.SemaphoreType.DMA((count + slots,)),
        ],
        cost_estimate=cost(2**24, blocks.size * 4),
        compiler_params=ROOM,
        name="far",
    )(row, links, *parents, blocks)


def far_bits(far):
    total = sum(piece.shape[0] for piece in far) // far[0].shape[0]
    return total.bit_length() - 1


def reversed_bits(at, bits):
    return sum(((at >> b) & 1) << (bits - 1 - b) for b in range(bits))


def back(tables, n, first, rank, blocks, links, messages, near, coupled, far, transfer, basis, start):
    final = start is not None
    arrived = len(messages)
    parts = [p for message in messages for p in message]
    part = parts[0].shape[0]
    count = len(far)
    bits = far_bits(far)
    operands = parts + [near, coupled, transfer, basis] + list(far) + ([start] if final else [])

    def body(*refs):
        tables_in, rank_ref, blocks_ref, links_ref, refs = refs[:4], refs[4], refs[5], refs[6], refs[7:]
        near_in, coupled_in, transfer_in, basis_in = refs[2 * arrived : 2 * arrived + 4]
        far_refs = refs[2 * arrived + 4 : 2 * arrived + 4 + count]
        out_ref, *rest = refs[len(operands) :]
        if final:
            past_ref = rest.pop(-2)
        else:
            top_ref = rest.pop(0)
        *held, transfer_ref, basis_ref, spread_ref, combined_ref, sems = rest
        copies = Copies(sems)
        base = [copies.start(near_in, out_ref), copies.start(coupled_in, combined_ref)]
        work = take_all(
            tables_in, n, first, arrived, copies, blocks_ref, links_ref, refs[: 2 * arrived], held,
            out_ref, combined_ref,
        )
        next(work)
        rows = far_refs[0].shape[0]
        late = []
        at = 0
        for ref in far_refs:
            for piece in range(ref.shape[0] // rows):
                share = share_of(jnp.bitwise_xor(tables_in[0][0], reversed_bits(at, bits)), bits)
                late.append(
                    copies.start(
                        ref.at[pl.ds(piece * rows, rows)],
                        spread_ref.at[pl.ds(pl.multiple_of(share * rows, rows), rows)],
                    )
                )
                at += 1
        late.append(copies.start(transfer_in, transfer_ref))
        late.append(copies.start(basis_in, basis_ref))
        if final:
            late.append(copies.start(refs[len(operands) - 1], past_ref))
        for copy in base:
            copy.wait()
        for _ in work:
            pass

        for copy in late:
            copy.wait()
        combined_ref[...] += contract2(transfer_ref[...], spread_ref[...], NT)
        row = lax.broadcasted_iota(jnp.int32, combined_ref.shape, 0)
        combined = jnp.where(row < rank_ref[0], combined_ref[...], 0.0)
        value = out_ref[...] + contract3(basis_ref[...], combined, NN)
        if final:
            out_ref[...] = 2.0 * value - past_ref[...]
        else:
            out_ref[...] = value
            top_ref[...] = value[:part, :].astype(BF16)

    out = jax.ShapeDtypeStruct(near.shape, F32)
    outs = (out,) if final else (out, jax.ShapeDtypeStruct(parts[0].shape, BF16))
    return pl.pallas_call(
        body,
        out_shape=outs,
        in_specs=[SMEM] * 5
        + [HBM] * 2
        + [ANY] * (2 * arrived + 2)
        + [HBM] * 2
        + [ANY] * count
        + ([HBM] if final else []),
        out_specs=(VMEM,) * len(outs),
        scratch_shapes=held_scratch(blocks, links, parts[0])
        + [
            pltpu.VMEM(transfer.shape, F32),
            pltpu.VMEM(basis.shape, F32),
            pltpu.VMEM((near.shape[1], transfer.shape[1]), BF16),
            pltpu.VMEM(coupled.shape, F32),
        ]
        + ([pltpu.VMEM(near.shape, F32)] if final else [])
        + [pltpu.SemaphoreType.DMA((4 * arrived + 5 + (1 << bits),))],
        cost_estimate=cost(6 * (blocks.shape[1] ** 2) * near.shape[1], 6 * (blocks.shape[1] ** 2)),
        compiler_params=ROOM,
        name="back",
    )(*tables, rank, blocks, links, *operands)


def local(
    probes,
    near_blocks,
    near_leaves,
    near_count,
    leaf_rank,
    leaf_basis,
    leaf_transfer,
    leaf_links,
    leaf_link_blocks,
    parent_links,
    parent_link_blocks,
):
    n = lax.axis_size("col")
    span_row = lax.axis_size("row")
    me = lax.axis_index("col")
    my_row = lax.axis_index("row")
    leaf_rows, _ = probes.shape
    keep = lambda a: pltpu.with_memory_space_constraint(a, pltpu.HBM)
    transfer = keep(leaf_transfer[0])
    blocks = keep(near_blocks[0])
    link_blocks = keep(leaf_link_blocks[0])
    parent_blocks = keep(parent_link_blocks[0])
    leaf_basis = keep(leaf_basis)
    past = keep(probes)
    bits = n.bit_length() - 1
    assert 1 << bits == n

    order = ring_order(n)
    to_right = [(order[i], order[(i + 1) % n]) for i in range(n)]
    to_left = [(b, a) for a, b in to_right]
    steps = n // 2 - 1

    mine = jnp.reshape(me, (1,))
    tables = (mine, near_leaves, near_count, leaf_links)

    def swap(value, axis, size, distance):
        return lax.ppermute(value, axis, [(i, i ^ distance) for i in range(size)])

    def pass_on(value, perm):
        return lax.ppermute(value, "col", perm)

    def multiply(vector, top, start):
        bottom, away, kept = front(mine, keep(vector), leaf_basis, transfer, leaf_rank)

        for b in range(bits):
            if b:
                pair = total.reshape(2, total.shape[0] // 2, total.shape[1])
                bit = (me >> b) & 1
                away = lax.dynamic_index_in_dim(pair, 1 - bit, 0, False).astype(BF16)
                kept = lax.dynamic_index_in_dim(pair, bit, 0, False)
            came = swap(away, "col", n, 1 << b)
            total = kept + came.astype(F32)
        share = total.astype(BF16)
        parents = [share] + [swap(share, "row", span_row, e) for e in range(1, span_row)]
        far = [far_share(jnp.reshape(my_row, (1,)), parent_links, parents, parent_blocks)]
        for b in reversed(range(bits)):
            held = far[0] if len(far) == 1 else jnp.concatenate(far)
            far.append(swap(held, "col", n, 1 << b))

        messages = [(top, bottom)]
        right = left = (top, bottom)
        for _ in range(1, steps + 1):
            right = tuple(pass_on(right[c], to_right) for c in (0, 1))
            left = tuple(pass_on(left[c], to_left) for c in (0, 1))
            messages += [right, left]
        opposite = (pass_on(right[0], to_right), pass_on(left[1], to_left))
        sums = absorb(tables, n, 0, blocks, link_blocks, [(top, keep(bottom))], ())
        first = 1
        for s in range(1, steps + 1):
            taken = messages[first : 2 * s + 1]
            sums = absorb(tables, n, first, blocks, link_blocks, taken, sums)
            first = 2 * s + 1
        return back(
            tables, n, first, leaf_rank, blocks, link_blocks, messages[first:] + [opposite],
            *sums, far, transfer, leaf_basis, start,
        )

    part = (leaf_rows + leaf_basis.shape[1]) // 2
    term_one, top = multiply(probes, probes[:part].astype(BF16), None)
    (term_two,) = multiply(term_one, top, past)
    return (term_one, term_two)


def solution(mesh):
    in_specs = (
        P(("row", "col"), None),
        P(("row", "col"), None, None, None),
        P(("row", "col"), None),
        P(("row", "col")),
        P(("row", "col")),
        P(("row", "col"), None),
        P(("row", "col"), None, None),
        P(("row", "col"), None),
        P(("row", "col"), None, None, None),
        P("row", None),
        P("row", None, None, None),
    )
    out_specs = (P(("row", "col"), None), P(("row", "col"), None))
    return jax.shard_map(local, mesh=mesh, in_specs=in_specs, out_specs=out_specs, check_vma=False)
```

```python
import jax
import jax.numpy as jnp
from jax import lax
from jax.experimental import pallas as pl
from jax.experimental.pallas import tpu as pltpu
from jax.sharding import PartitionSpec as P


F32 = jnp.float32
BF16 = jnp.bfloat16
VMEM = pl.BlockSpec(memory_space=pltpu.VMEM)
SMEM = pl.BlockSpec(memory_space=pltpu.SMEM)
HBM = pl.BlockSpec(memory_space=pltpu.HBM)
ANY = pl.BlockSpec(memory_space=pl.ANY)
ROOM = pltpu.CompilerParams(vmem_limit_bytes=24 * 2**20)


def ring_order(n):
    return list(range(0, n, 2)) + list(range(n - 1, 0, -2))


def halves(x):
    high = x.astype(BF16)
    low = (x - high.astype(F32)).astype(BF16)
    return high, low


def contract(a, b, dims):
    return lax.dot_general(a, b, (dims, ((), ())), preferred_element_type=F32)


def contract3(a, b, dims):
    a_high, a_low = halves(a)
    b_high, b_low = halves(b)
    small = contract(a_low, b_high, dims) + contract(a_high, b_low, dims)
    return small + contract(a_high, b_high, dims)


def contract2(a, b, dims):
    a_high, a_low = halves(a)
    return contract(a_low, b, dims) + contract(a_high, b, dims)


NN = ((1,), (0,))
NT = ((1,), (1,))
TN = ((0,), (0,))


def cost(flops, moved):
    return pl.CostEstimate(flops=int(flops), bytes_accessed=int(moved), transcendentals=0)


def share_of(me, bits):
    share = me & 1
    for b in range(1, bits):
        share = 2 * share + ((me >> b) & 1)
    return share


SHARE = 5
DEPTH = 3


class Copies:
    def __init__(self, sems):
        self.sems = sems
        self.made = []

    def start(self, source, target, when=None):
        copy = pltpu.make_async_copy(source, target, self.sems.at[len(self.made)])
        self.made.append(copy)
        if when is None:
            copy.start()
        else:
            pl.when(when)(copy.start)
        return copy


def front(me, v, basis, transfer, rank, split):
    leaf_rows, probe_cols = v.shape
    rank_cols, parent_cols = transfer.shape
    half = probe_cols // 2

    def body(me_ref, rank_ref, v_in, basis_in, transfer_in, bottom_ref, away_ref, kept_ref, v_ref, basis_ref, transfer_ref, upward_ref, sems):
        copies = Copies(sems)
        first = [copies.start(v_in, v_ref), copies.start(basis_in, basis_ref)]
        last = copies.start(transfer_in, transfer_ref)
        for copy in first:
            copy.wait()
        v = v_ref[...]
        skeleton = contract3(basis_ref[...], v, TN)
        row = lax.broadcasted_iota(jnp.int32, skeleton.shape, 0)
        skeleton = jnp.where(row < rank_ref[0], skeleton, 0.0)
        bottom_ref[: leaf_rows - split, :] = v[split:, :].astype(BF16)
        bottom_ref[leaf_rows - split :, :] = skeleton.astype(BF16)
        last.wait()
        upward_ref[...] = contract3(skeleton, transfer_ref[...], TN)
        bit = me_ref[0] & 1
        away_ref[...] = upward_ref[pl.ds(pl.multiple_of((1 - bit) * half, half), half), :].astype(BF16)
        kept_ref[...] = upward_ref[pl.ds(pl.multiple_of(bit * half, half), half), :]

    return pl.pallas_call(
        body,
        out_shape=(
            jax.ShapeDtypeStruct((leaf_rows + rank_cols - split, probe_cols), BF16),
            jax.ShapeDtypeStruct((half, parent_cols), BF16),
            jax.ShapeDtypeStruct((half, parent_cols), F32),
        ),
        in_specs=[SMEM, SMEM, HBM, HBM, HBM],
        out_specs=(VMEM,) * 3,
        scratch_shapes=[
            pltpu.VMEM(v.shape, F32),
            pltpu.VMEM(basis.shape, F32),
            pltpu.VMEM(transfer.shape, F32),
            pltpu.VMEM((probe_cols, parent_cols), F32),
            pltpu.SemaphoreType.DMA((3,)),
        ],
        cost_estimate=cost(6 * v.size * rank_cols, 8 * v.size),
        compiler_params=ROOM,
        name="front",
    )(me, rank, v, basis, transfer)


def origin(me, j, n):
    place = jnp.where(me & 1 == 1, n - ((me + 1) >> 1), me >> 1)
    step = (j + 1) // 2
    place = place - step if j % 2 else place + step
    place = jnp.where(place < 0, place + n, jnp.where(place >= n, place - n, place))
    return jnp.where(place < n // 2, 2 * place, 2 * (n - place) - 1)


def named(me_ref, near_ref, count_ref, links_ref, j, n):
    leaf = origin(me_ref[0], j, n)
    slot = jnp.int32(-1)
    for k in range(near_ref.shape[1]):
        slot = jnp.where((near_ref[0, k] == leaf) & (k < count_ref[0]), k, slot)
    link = jnp.int32(-1)
    for k in range(links_ref.shape[1]):
        link = jnp.where(links_ref[0, k] == leaf, k, link)
    return slot >= 0, jnp.maximum(slot, 0), link >= 0, jnp.maximum(link, 0)


def take_all(tables, n, first, count, copies, blocks_ref, links_ref, parts, held, near_ref, coupled_ref):
    block_ref, link_ref, held_ref = held
    split = parts[0].shape[0]
    rows = (pl.ds(0, split), pl.ds(split, parts[1].shape[0]))
    leaf_rows = near_ref.shape[0]

    def fetch(j):
        at = j % DEPTH
        live, slot, linked, link = named(*tables, first + j, n)
        got = [copies.start(parts[2 * j + c], held_ref.at[at, rows[c]]) for c in (0, 1)]
        block = copies.start(blocks_ref.at[slot], block_ref.at[at], live)
        tie = copies.start(links_ref.at[link], link_ref.at[at], linked)
        return live, linked, got, block, tie

    fetched = [fetch(j) for j in range(min(count, DEPTH - 1))]
    yield
    for j in range(count):
        live, linked, got, block, tie = fetched[j]
        at = j % DEPTH
        for copy in got:
            copy.wait()
        pl.when(live)(block.wait)
        if j + DEPTH - 1 < count:
            fetched.append(fetch(j + DEPTH - 1))
        yield

        @pl.when(live)
        def _():
            near_ref[...] += contract(block_ref[at], held_ref[at, :leaf_rows, :], NN)

        @pl.when(linked)
        def _():
            tie.wait()
            coupled_ref[...] += contract2(link_ref[at], held_ref[at, leaf_rows:, :], NN)


def held_scratch(blocks, links, message):
    return [
        pltpu.VMEM((DEPTH,) + blocks.shape[1:], BF16),
        pltpu.VMEM((DEPTH,) + links.shape[1:], F32),
        pltpu.VMEM((DEPTH, sum(part.shape[0] for part in message), message[0].shape[1]), BF16),
    ]


def absorb(tables, n, first, blocks, links, messages, sums):
    probe_cols = messages[0][0].shape[1]
    count = len(messages)
    outs = (
        jax.ShapeDtypeStruct((blocks.shape[1], probe_cols), F32),
        jax.ShapeDtypeStruct((links.shape[1], probe_cols), F32),
    )
    operands = [p for message in messages for p in message] + list(sums)

    def body(*refs):
        tables_in, blocks_ref, links_ref, refs = refs[:4], refs[4], refs[5], refs[6:]
        near_out, coupled_out, *held, sems = refs[len(operands) :]
        copies = Copies(sems)
        base = [
            copies.start(given, out)
            for given, out in zip(refs[2 * count : len(operands)], (near_out, coupled_out))
        ]
        work = take_all(
            tables_in, n, first, count, copies, blocks_ref, links_ref, refs[: 2 * count], held,
            near_out, coupled_out,
        )
        next(work)
        if sums:
            for copy in base:
                copy.wait()
        else:
            near_out[...] = jnp.zeros_like(near_out)
            coupled_out[...] = jnp.zeros_like(coupled_out)
        for _ in work:
            pass

    return pl.pallas_call(
        body,
        out_shape=outs,
        in_specs=[SMEM] * 4 + [HBM] * 2 + [ANY] * len(operands),
        out_specs=(VMEM, VMEM),
        scratch_shapes=held_scratch(blocks, links, messages[0])
        + [pltpu.SemaphoreType.DMA((4 * count + 2,))],
        cost_estimate=cost(2 * count * (blocks.shape[1] ** 2) * probe_cols, 4 * count * (blocks.shape[1] ** 2)),
        compiler_params=ROOM,
        name="absorb",
    )(*tables, blocks, links, *operands)


def far_share(row, links, parents, blocks):
    count = len(parents)
    slots = blocks.shape[0]

    def body(row_ref, links_ref, *refs):
        blocks_in, out_ref, blocks_ref, parents_ref, sems = refs[count:]
        copies = Copies(sems)
        brought = [copies.start(refs[e], parents_ref.at[e]) for e in range(count)]
        fetched = [copies.start(blocks_in.at[k], blocks_ref.at[k]) for k in range(slots)]
        for copy in brought:
            copy.wait()
        total = jnp.zeros(out_ref.shape, F32)
        for k in range(slots):
            away = jnp.bitwise_xor(links_ref[0, k], row_ref[0])
            chosen = parents_ref[away]
            fetched[k].wait()
            high, low = halves(blocks_ref[k])
            total += contract(chosen, low, NT) + contract(chosen, high, NT)
        out_ref[...] = total.astype(BF16)

    return pl.pallas_call(
        body,
        out_shape=jax.ShapeDtypeStruct(parents[0].shape, BF16),
        in_specs=[SMEM, SMEM] + [ANY] * count + [HBM],
        out_specs=VMEM,
        scratch_shapes=[
            pltpu.VMEM(blocks.shape, F32),
            pltpu.VMEM((count,) + parents[0].shape, BF16),
            pltpu.SemaphoreType.DMA((count + slots,)),
        ],
        cost_estimate=cost(2**24, blocks.size * 4),
        compiler_params=ROOM,
        name="far",
    )(row, links, *parents, blocks)


def far_bits(far):
    total = sum(piece.shape[0] for piece in far) // far[0].shape[0]
    return total.bit_length() - 1


def reversed_bits(at, bits):
    return sum(((at >> b) & 1) << (bits - 1 - b) for b in range(bits))


def back(tables, n, first, rank, blocks, links, messages, near, coupled, far, transfer, basis, start):
    final = start is not None
    arrived = len(messages)
    parts = [p for message in messages for p in message]
    part = parts[0].shape[0]
    count = len(far)
    bits = far_bits(far)
    operands = parts + [near, coupled, transfer, basis] + list(far) + ([start] if final else [])

    def body(*refs):
        tables_in, rank_ref, blocks_ref, links_ref, refs = refs[:4], refs[4], refs[5], refs[6], refs[7:]
        near_in, coupled_in, transfer_in, basis_in = refs[2 * arrived : 2 * arrived + 4]
        far_refs = refs[2 * arrived + 4 : 2 * arrived + 4 + count]
        out_ref, *rest = refs[len(operands) :]
        if final:
            past_ref = rest.pop(-2)
        else:
            top_ref = rest.pop(0)
        *held, transfer_ref, basis_ref, spread_ref, combined_ref, sems = rest
        copies = Copies(sems)
        base = [copies.start(near_in, out_ref), copies.start(coupled_in, combined_ref)]
        work = take_all(
            tables_in, n, first, arrived, copies, blocks_ref, links_ref, refs[: 2 * arrived], held,
            out_ref, combined_ref,
        )
        next(work)
        rows = far_refs[0].shape[0]
        late = []
        at = 0
        for ref in far_refs:
            for piece in range(ref.shape[0] // rows):
                share = share_of(jnp.bitwise_xor(tables_in[0][0], reversed_bits(at, bits)), bits)
                late.append(
                    copies.start(
                        ref.at[pl.ds(piece * rows, rows)],
                        spread_ref.at[pl.ds(pl.multiple_of(share * rows, rows), rows)],
                    )
                )
                at += 1
        late.append(copies.start(transfer_in, transfer_ref))
        late.append(copies.start(basis_in, basis_ref))
        if final:
            late.append(copies.start(refs[len(operands) - 1], past_ref))
        for copy in base:
            copy.wait()
        for _ in work:
            pass

        for copy in late:
            copy.wait()
        combined_ref[...] += contract2(transfer_ref[...], spread_ref[...], NT)
        row = lax.broadcasted_iota(jnp.int32, combined_ref.shape, 0)
        combined = jnp.where(row < rank_ref[0], combined_ref[...], 0.0)
        value = out_ref[...] + contract3(basis_ref[...], combined, NN)
        if final:
            out_ref[...] = 2.0 * value - past_ref[...]
        else:
            out_ref[...] = value
            top_ref[...] = value[:part, :].astype(BF16)

    out = jax.ShapeDtypeStruct(near.shape, F32)
    outs = (out,) if final else (out, jax.ShapeDtypeStruct(parts[0].shape, BF16))
    return pl.pallas_call(
        body,
        out_shape=outs,
        in_specs=[SMEM] * 5
        + [HBM] * 2
        + [ANY] * (2 * arrived + 2)
        + [HBM] * 2
        + [ANY] * count
        + ([HBM] if final else []),
        out_specs=(VMEM,) * len(outs),
        scratch_shapes=held_scratch(blocks, links, messages[0])
        + [
            pltpu.VMEM(transfer.shape, F32),
            pltpu.VMEM(basis.shape, F32),
            pltpu.VMEM((near.shape[1], transfer.shape[1]), BF16),
            pltpu.VMEM(coupled.shape, F32),
        ]
        + ([pltpu.VMEM(near.shape, F32)] if final else [])
        + [pltpu.SemaphoreType.DMA((4 * arrived + 5 + (1 << bits),))],
        cost_estimate=cost(6 * (blocks.shape[1] ** 2) * near.shape[1], 6 * (blocks.shape[1] ** 2)),
        compiler_params=ROOM,
        name="back",
    )(*tables, rank, blocks, links, *operands)


def local(
    probes,
    near_blocks,
    near_leaves,
    near_count,
    leaf_rank,
    leaf_basis,
    leaf_transfer,
    leaf_links,
    leaf_link_blocks,
    parent_links,
    parent_link_blocks,
):
    n = lax.axis_size("col")
    span_row = lax.axis_size("row")
    me = lax.axis_index("col")
    my_row = lax.axis_index("row")
    leaf_rows, _ = probes.shape
    keep = lambda a: pltpu.with_memory_space_constraint(a, pltpu.HBM)
    transfer = keep(leaf_transfer[0])
    blocks = keep(near_blocks[0])
    link_blocks = keep(leaf_link_blocks[0])
    parent_blocks = keep(parent_link_blocks[0])
    leaf_basis = keep(leaf_basis)
    past = keep(probes)
    bits = n.bit_length() - 1
    assert 1 << bits == n

    order = ring_order(n)
    to_right = [(order[i], order[(i + 1) % n]) for i in range(n)]
    to_left = [(b, a) for a, b in to_right]
    steps = n // 2 - 1

    mine = jnp.reshape(me, (1,))
    tables = (mine, near_leaves, near_count, leaf_links)

    def swap(value, axis, size, distance):
        return lax.ppermute(value, axis, [(i, i ^ distance) for i in range(size)])

    def pass_on(value, perm):
        return lax.ppermute(value, "col", perm)

    def multiply(vector, top, start):
        bottom, away, kept = front(mine, keep(vector), leaf_basis, transfer, leaf_rank, top.shape[0])

        for b in range(bits):
            if b:
                pair = total.reshape(2, total.shape[0] // 2, total.shape[1])
                bit = (me >> b) & 1
                away = lax.dynamic_index_in_dim(pair, 1 - bit, 0, False).astype(BF16)
                kept = lax.dynamic_index_in_dim(pair, bit, 0, False)
            came = swap(away, "col", n, 1 << b)
            total = kept + came.astype(F32)
        share = total.astype(BF16)
        parents = [share] + [swap(share, "row", span_row, e) for e in range(1, span_row)]
        far = [far_share(jnp.reshape(my_row, (1,)), parent_links, parents, parent_blocks)]
        for b in reversed(range(bits)):
            held = far[0] if len(far) == 1 else jnp.concatenate(far)
            far.append(swap(held, "col", n, 1 << b))

        messages = [(top, bottom)]
        right = left = (top, bottom)
        for _ in range(1, steps + 1):
            right = tuple(pass_on(right[c], to_right) for c in (0, 1))
            left = tuple(pass_on(left[c], to_left) for c in (0, 1))
            messages += [right, left]
        opposite = (pass_on(right[0], to_right), pass_on(left[1], to_left))
        sums = absorb(tables, n, 0, blocks, link_blocks, [(top, keep(bottom))], ())
        sums = absorb(tables, n, 1, blocks, link_blocks, messages[1:-2], sums)
        sums = absorb(tables, n, n - 3, blocks, link_blocks, messages[-2:], sums)
        first = n - 1
        return back(
            tables, n, first, leaf_rank, blocks, link_blocks, messages[first:] + [opposite],
            *sums, far, transfer, leaf_basis, start,
        )

    split = (leaf_rows + leaf_basis.shape[1]) * SHARE // 10 // 128 * 128
    term_one, top = multiply(probes, probes[:split].astype(BF16), None)
    (term_two,) = multiply(term_one, top, past)
    return (term_one, term_two)


def solution(mesh):
    in_specs = (
        P(("row", "col"), None),
        P(("row", "col"), None, None, None),
        P(("row", "col"), None),
        P(("row", "col")),
        P(("row", "col")),
        P(("row", "col"), None),
        P(("row", "col"), None, None),
        P(("row", "col"), None),
        P(("row", "col"), None, None, None),
        P("row", None),
        P("row", None, None, None),
    )
    out_specs = (P(("row", "col"), None), P(("row", "col"), None))
    return jax.shard_map(local, mesh=mesh, in_specs=in_specs, out_specs=out_specs, check_vma=False)
```

```python
import jax
import jax.numpy as jnp
from jax import lax
from jax.experimental import pallas as pl
from jax.experimental.pallas import tpu as pltpu
from jax.sharding import PartitionSpec as P


F32 = jnp.float32
BF16 = jnp.bfloat16
VMEM = pl.BlockSpec(memory_space=pltpu.VMEM)
SMEM = pl.BlockSpec(memory_space=pltpu.SMEM)
HBM = pl.BlockSpec(memory_space=pltpu.HBM)
ANY = pl.BlockSpec(memory_space=pl.ANY)
ROOM = pltpu.CompilerParams(vmem_limit_bytes=24 * 2**20)


def ring_order(n):
    return list(range(0, n, 2)) + list(range(n - 1, 0, -2))


def halves(x):
    high = x.astype(BF16)
    low = (x - high.astype(F32)).astype(BF16)
    return high, low


def contract(a, b, dims):
    return lax.dot_general(a, b, (dims, ((), ())), preferred_element_type=F32)


def contract3(a, b, dims):
    a_high, a_low = halves(a)
    b_high, b_low = halves(b)
    small = contract(a_low, b_high, dims) + contract(a_high, b_low, dims)
    return small + contract(a_high, b_high, dims)


def contract2(a, b, dims):
    a_high, a_low = halves(a)
    return contract(a_low, b, dims) + contract(a_high, b, dims)


NN = ((1,), (0,))
NT = ((1,), (1,))
TN = ((0,), (0,))


def cost(flops, moved):
    return pl.CostEstimate(flops=int(flops), bytes_accessed=int(moved), transcendentals=0)


def share_of(me, bits):
    share = me & 1
    for b in range(1, bits):
        share = 2 * share + ((me >> b) & 1)
    return share


SHARE = 5
DEPTH = 3


class Copies:
    def __init__(self, sems):
        self.sems = sems
        self.made = []

    def start(self, source, target, when=None):
        copy = pltpu.make_async_copy(source, target, self.sems.at[len(self.made)])
        self.made.append(copy)
        if when is None:
            copy.start()
        else:
            pl.when(when)(copy.start)
        return copy


def front(me, v, basis, transfer, rank, split):
    leaf_rows, probe_cols = v.shape
    rank_cols, parent_cols = transfer.shape
    half = probe_cols // 2

    def body(me_ref, rank_ref, v_in, basis_in, transfer_in, bottom_ref, away_ref, kept_ref, v_ref, basis_ref, transfer_ref, upward_ref, sems):
        copies = Copies(sems)
        first = [copies.start(v_in, v_ref), copies.start(basis_in, basis_ref)]
        last = copies.start(transfer_in, transfer_ref)
        for copy in first:
            copy.wait()
        v = v_ref[...]
        skeleton = contract3(basis_ref[...], v, TN)
        row = lax.broadcasted_iota(jnp.int32, skeleton.shape, 0)
        skeleton = jnp.where(row < rank_ref[0], skeleton, 0.0)
        bottom_ref[: leaf_rows - split, :] = v[split:, :].astype(BF16)
        bottom_ref[leaf_rows - split :, :] = skeleton.astype(BF16)
        last.wait()
        upward_ref[...] = contract3(skeleton, transfer_ref[...], TN)
        bit = me_ref[0] & 1
        away_ref[...] = upward_ref[pl.ds(pl.multiple_of((1 - bit) * half, half), half), :].astype(BF16)
        kept_ref[...] = upward_ref[pl.ds(pl.multiple_of(bit * half, half), half), :]

    return pl.pallas_call(
        body,
        out_shape=(
            jax.ShapeDtypeStruct((leaf_rows + rank_cols - split, probe_cols), BF16),
            jax.ShapeDtypeStruct((half, parent_cols), BF16),
            jax.ShapeDtypeStruct((half, parent_cols), F32),
        ),
        in_specs=[SMEM, SMEM, HBM, HBM, HBM],
        out_specs=(VMEM,) * 3,
        scratch_shapes=[
            pltpu.VMEM(v.shape, F32),
            pltpu.VMEM(basis.shape, F32),
            pltpu.VMEM(transfer.shape, F32),
            pltpu.VMEM((probe_cols, parent_cols), F32),
            pltpu.SemaphoreType.DMA((3,)),
        ],
        cost_estimate=cost(6 * v.size * rank_cols, 8 * v.size),
        compiler_params=ROOM,
        name="front",
    )(me, rank, v, basis, transfer)


def origin(me, j, n):
    place = jnp.where(me & 1 == 1, n - ((me + 1) >> 1), me >> 1)
    step = (j + 1) // 2
    place = place - step if j % 2 else place + step
    place = jnp.where(place < 0, place + n, jnp.where(place >= n, place - n, place))
    return jnp.where(place < n // 2, 2 * place, 2 * (n - place) - 1)


def named(me_ref, near_ref, count_ref, links_ref, j, n):
    leaf = origin(me_ref[0], j, n)
    slot = jnp.int32(-1)
    for k in range(near_ref.shape[1]):
        slot = jnp.where((near_ref[0, k] == leaf) & (k < count_ref[0]), k, slot)
    link = jnp.int32(-1)
    for k in range(links_ref.shape[1]):
        link = jnp.where(links_ref[0, k] == leaf, k, link)
    return slot >= 0, jnp.maximum(slot, 0), link >= 0, jnp.maximum(link, 0)


def take_all(tables, n, first, count, copies, blocks_ref, links_ref, parts, held, near_ref, coupled_ref):
    block_ref, link_ref, held_ref = held
    split = parts[0].shape[0]
    rows = (pl.ds(0, split), pl.ds(split, parts[1].shape[0]))
    leaf_rows = near_ref.shape[0]

    def fetch(j):
        at = j % DEPTH
        live, slot, linked, link = named(*tables, first + j, n)
        got = [copies.start(parts[2 * j + c], held_ref.at[at, rows[c]]) for c in (0, 1)]
        block = copies.start(blocks_ref.at[slot], block_ref.at[at], live)
        tie = coupled_ref is not None and copies.start(links_ref.at[link], link_ref.at[at], linked)
        return live, linked, got, block, tie

    fetched = [fetch(j) for j in range(min(count, DEPTH - 1))]
    yield
    for j in range(count):
        live, linked, got, block, tie = fetched[j]
        at = j % DEPTH
        for copy in got:
            copy.wait()
        pl.when(live)(block.wait)
        if j + DEPTH - 1 < count:
            fetched.append(fetch(j + DEPTH - 1))
        yield

        @pl.when(live)
        def _():
            near_ref[...] += contract(block_ref[at], held_ref[at, :leaf_rows, :], NN)

        if coupled_ref is None:
            continue

        @pl.when(linked)
        def _():
            tie.wait()
            coupled_ref[...] += contract2(link_ref[at], held_ref[at, leaf_rows:, :], NN)


def held_scratch(blocks, links, message):
    return [
        pltpu.VMEM((DEPTH,) + blocks.shape[1:], BF16),
        pltpu.VMEM((DEPTH,) + links.shape[1:], F32),
        pltpu.VMEM((DEPTH, sum(part.shape[0] for part in message), message[0].shape[1]), BF16),
    ]


def absorb(tables, n, first, blocks, links, messages, sums):
    probe_cols = messages[0][0].shape[1]
    count = len(messages)
    outs = (
        jax.ShapeDtypeStruct((blocks.shape[1], probe_cols), F32),
        jax.ShapeDtypeStruct((links.shape[1], probe_cols), F32),
    )
    operands = [p for message in messages for p in message] + list(sums)

    def body(*refs):
        tables_in, blocks_ref, links_ref, refs = refs[:4], refs[4], refs[5], refs[6:]
        near_out, *rest = refs[len(operands) :]
        coupled_out = rest.pop(0) if sums else None
        *held, sems = rest
        copies = Copies(sems)
        base = [
            copies.start(given, out)
            for given, out in zip(refs[2 * count : len(operands)], (near_out, coupled_out))
        ]
        work = take_all(
            tables_in, n, first, count, copies, blocks_ref, links_ref, refs[: 2 * count], held,
            near_out, coupled_out,
        )
        next(work)
        for copy in base:
            copy.wait()
        if len(sums) < 1:
            near_out[...] = jnp.zeros_like(near_out)
        elif len(sums) < 2:
            coupled_out[...] = jnp.zeros_like(coupled_out)
        for _ in work:
            pass

    return pl.pallas_call(
        body,
        out_shape=outs if sums else outs[:1],
        in_specs=[SMEM] * 4 + [HBM] * 2 + [ANY] * len(operands),
        out_specs=(VMEM, VMEM) if sums else (VMEM,),
        scratch_shapes=held_scratch(blocks, links, messages[0])
        + [pltpu.SemaphoreType.DMA((4 * count + 2,))],
        cost_estimate=cost(2 * count * (blocks.shape[1] ** 2) * probe_cols, 4 * count * (blocks.shape[1] ** 2)),
        compiler_params=ROOM,
        name="absorb",
    )(*tables, blocks, links, *operands)


def far_share(row, links, parents, blocks):
    count = len(parents)
    slots = blocks.shape[0]

    def body(row_ref, links_ref, *refs):
        blocks_in, out_ref, blocks_ref, parents_ref, sems = refs[count:]
        copies = Copies(sems)
        brought = [copies.start(refs[e], parents_ref.at[e]) for e in range(count)]
        fetched = [copies.start(blocks_in.at[k], blocks_ref.at[k]) for k in range(slots)]
        for copy in brought:
            copy.wait()
        total = jnp.zeros(out_ref.shape, F32)
        for k in range(slots):
            away = jnp.bitwise_xor(links_ref[0, k], row_ref[0])
            chosen = parents_ref[away]
            fetched[k].wait()
            high, low = halves(blocks_ref[k])
            total += contract(chosen, low, NT) + contract(chosen, high, NT)
        out_ref[...] = total.astype(BF16)

    return pl.pallas_call(
        body,
        out_shape=jax.ShapeDtypeStruct(parents[0].shape, BF16),
        in_specs=[SMEM, SMEM] + [ANY] * count + [HBM],
        out_specs=VMEM,
        scratch_shapes=[
            pltpu.VMEM(blocks.shape, F32),
            pltpu.VMEM((count,) + parents[0].shape, BF16),
            pltpu.SemaphoreType.DMA((count + slots,)),
        ],
        cost_estimate=cost(2**24, blocks.size * 4),
        compiler_params=ROOM,
        name="far",
    )(row, links, *parents, blocks)


def far_bits(far):
    total = sum(piece.shape[0] for piece in far) // far[0].shape[0]
    return total.bit_length() - 1


def reversed_bits(at, bits):
    return sum(((at >> b) & 1) << (bits - 1 - b) for b in range(bits))


def back(tables, n, first, rank, blocks, links, messages, near, coupled, far, transfer, basis, start):
    final = start is not None
    arrived = len(messages)
    parts = [p for message in messages for p in message]
    part = parts[0].shape[0]
    count = len(far)
    bits = far_bits(far)
    operands = parts + [near, coupled, transfer, basis] + list(far) + ([start] if final else [])

    def body(*refs):
        tables_in, rank_ref, blocks_ref, links_ref, refs = refs[:4], refs[4], refs[5], refs[6], refs[7:]
        near_in, coupled_in, transfer_in, basis_in = refs[2 * arrived : 2 * arrived + 4]
        far_refs = refs[2 * arrived + 4 : 2 * arrived + 4 + count]
        out_ref, *rest = refs[len(operands) :]
        if final:
            past_ref = rest.pop(-2)
        else:
            top_ref = rest.pop(0)
        *held, transfer_ref, basis_ref, spread_ref, combined_ref, sems = rest
        copies = Copies(sems)
        base = [copies.start(near_in, out_ref), copies.start(coupled_in, combined_ref)]
        work = take_all(
            tables_in, n, first, arrived, copies, blocks_ref, links_ref, refs[: 2 * arrived], held,
            out_ref, combined_ref,
        )
        next(work)
        rows = far_refs[0].shape[0]
        late = []
        at = 0
        for ref in far_refs:
            for piece in range(ref.shape[0] // rows):
                share = share_of(jnp.bitwise_xor(tables_in[0][0], reversed_bits(at, bits)), bits)
                late.append(
                    copies.start(
                        ref.at[pl.ds(piece * rows, rows)],
                        spread_ref.at[pl.ds(pl.multiple_of(share * rows, rows), rows)],
                    )
                )
                at += 1
        late.append(copies.start(transfer_in, transfer_ref))
        late.append(copies.start(basis_in, basis_ref))
        if final:
            late.append(copies.start(refs[len(operands) - 1], past_ref))
        for copy in base:
            copy.wait()
        for _ in work:
            pass

        for copy in late:
            copy.wait()
        combined_ref[...] += contract2(transfer_ref[...], spread_ref[...], NT)
        row = lax.broadcasted_iota(jnp.int32, combined_ref.shape, 0)
        combined = jnp.where(row < rank_ref[0], combined_ref[...], 0.0)
        value = out_ref[...] + contract3(basis_ref[...], combined, NN)
        if final:
            out_ref[...] = 2.0 * value - past_ref[...]
        else:
            out_ref[...] = value
            top_ref[...] = value[:part, :].astype(BF16)

    out = jax.ShapeDtypeStruct(near.shape, F32)
    outs = (out,) if final else (out, jax.ShapeDtypeStruct(parts[0].shape, BF16))
    return pl.pallas_call(
        body,
        out_shape=outs,
        in_specs=[SMEM] * 5
        + [HBM] * 2
        + [ANY] * (2 * arrived + 2)
        + [HBM] * 2
        + [ANY] * count
        + ([HBM] if final else []),
        out_specs=(VMEM,) * len(outs),
        scratch_shapes=held_scratch(blocks, links, messages[0])
        + [
            pltpu.VMEM(transfer.shape, F32),
            pltpu.VMEM(basis.shape, F32),
            pltpu.VMEM((near.shape[1], transfer.shape[1]), BF16),
            pltpu.VMEM(coupled.shape, F32),
        ]
        + ([pltpu.VMEM(near.shape, F32)] if final else [])
        + [pltpu.SemaphoreType.DMA((4 * arrived + 5 + (1 << bits),))],
        cost_estimate=cost(6 * (blocks.shape[1] ** 2) * near.shape[1], 6 * (blocks.shape[1] ** 2)),
        compiler_params=ROOM,
        name="back",
    )(*tables, rank, blocks, links, *operands)


def local(
    probes,
    near_blocks,
    near_leaves,
    near_count,
    leaf_rank,
    leaf_basis,
    leaf_transfer,
    leaf_links,
    leaf_link_blocks,
    parent_links,
    parent_link_blocks,
):
    n = lax.axis_size("col")
    span_row = lax.axis_size("row")
    me = lax.axis_index("col")
    my_row = lax.axis_index("row")
    leaf_rows, _ = probes.shape
    keep = lambda a: pltpu.with_memory_space_constraint(a, pltpu.HBM)
    transfer = keep(leaf_transfer[0])
    blocks = keep(near_blocks[0])
    link_blocks = keep(leaf_link_blocks[0])
    parent_blocks = keep(parent_link_blocks[0])
    leaf_basis = keep(leaf_basis)
    past = keep(probes)
    bits = n.bit_length() - 1
    assert 1 << bits == n

    order = ring_order(n)
    to_right = [(order[i], order[(i + 1) % n]) for i in range(n)]
    to_left = [(b, a) for a, b in to_right]
    steps = n // 2 - 1

    mine = jnp.reshape(me, (1,))
    tables = (mine, keep(near_leaves), near_count, keep(leaf_links))

    def swap(value, axis, size, distance):
        return lax.ppermute(value, axis, [(i, i ^ distance) for i in range(size)])

    def pass_on(value, perm):
        return lax.ppermute(value, "col", perm)

    def multiply(vector, top, start):
        bottom, away, kept = front(mine, keep(vector), leaf_basis, transfer, leaf_rank, top.shape[0])

        for b in range(bits):
            if b:
                pair = total.reshape(2, total.shape[0] // 2, total.shape[1])
                bit = (me >> b) & 1
                away = lax.dynamic_index_in_dim(pair, 1 - bit, 0, False).astype(BF16)
                kept = lax.dynamic_index_in_dim(pair, bit, 0, False)
            came = swap(away, "col", n, 1 << b)
            total = kept + came.astype(F32)
        share = total.astype(BF16)
        parents = [share] + [swap(share, "row", span_row, e) for e in range(1, span_row)]
        far = [far_share(jnp.reshape(my_row, (1,)), parent_links, parents, parent_blocks)]
        for b in reversed(range(bits)):
            held = far[0] if len(far) == 1 else jnp.concatenate(far)
            far.append(swap(held, "col", n, 1 << b))

        messages = [(top, bottom)]
        right = left = (top, bottom)
        for _ in range(1, steps + 1):
            right = tuple(pass_on(right[c], to_right) for c in (0, 1))
            left = tuple(pass_on(left[c], to_left) for c in (0, 1))
            messages += [right, left]
        opposite = (pass_on(right[0], to_right), pass_on(left[1], to_left))
        sums = absorb(tables, n, 0, blocks, link_blocks, [(top, keep(bottom))], ())
        sums = absorb(tables, n, 1, blocks, link_blocks, messages[1:-2], sums)
        sums = absorb(tables, n, n - 3, blocks, link_blocks, messages[-2:], sums)
        first = n - 1
        return back(
            tables, n, first, leaf_rank, blocks, link_blocks, messages[first:] + [opposite],
            *sums, far, transfer, leaf_basis, start,
        )

    split = (leaf_rows + leaf_basis.shape[1]) * SHARE // 10 // 128 * 128
    term_one, top = multiply(probes, probes[:split].astype(BF16), None)
    (term_two,) = multiply(term_one, top, past)
    return (term_one, term_two)


def solution(mesh):
    in_specs = (
        P(("row", "col"), None),
        P(("row", "col"), None, None, None),
        P(("row", "col"), None),
        P(("row", "col")),
        P(("row", "col")),
        P(("row", "col"), None),
        P(("row", "col"), None, None),
        P(("row", "col"), None),
        P(("row", "col"), None, None, None),
        P("row", None),
        P("row", None, None, None),
    )
    out_specs = (P(("row", "col"), None), P(("row", "col"), None))
    return jax.shard_map(local, mesh=mesh, in_specs=in_specs, out_specs=out_specs, check_vma=False)
```
